256 devices in a mesh: seq: 64 (over x_lo, y, z), sub: 4 (over x_hi, core).
Axes of the slice: x: 4 (x_hi: 2, x_lo: 2; x = x_hi * 2 + x_lo), y: 4, z: 8, core: 2. Of those that a mesh axis runs over, the one named last changes fastest.
Arguments:
- normed: bfloat16 [32768, 2048], P(('seq', 'sub')), as said below
- w_query: bfloat16 [2048, 2048], P(None, 'sub'), as said below
- w_key: bfloat16 [2048, 2048], P(None, 'sub'), as said below
- w_value: bfloat16 [2048, 2048], P(None, 'sub'), may hold values from -0.125 to 0.125
- w_out: bfloat16 [2048, 2048], P('sub'), may hold values from -0.25 to 0.25
- pattern: int32 [16, 128], P('sub'), may hold values from 0 to 127, each once within a row
- slide_lengths: int32 [8], replicated, may hold values from 1 to 160, 256 in all
Outputs:
- mixed: bfloat16 [32768, 2048], P(('seq', 'sub'))
The draws below stay inside these ranges and needn't reach their ends.
Inputs may be any that keep to these rules, and one draw needn't show every extreme that they name: `pattern`: each row is an ordering of the 128 positions of a block. `slide_lengths`: the slides lie end to end and fill all 256 blocks. `normed`: entries of order one. `w_query`: entries of order 2048 ** -0.5. `w_key`: entries of order 2048 ** -0.5.
All inputs are finite; a program needn't handle non-finite values.
Results may differ from the reference program's by a relative error of at most 0.012.
Values may be sent and summed in bfloat16 or wider, within the bound.
A program may use at most 128 MiB of HBM per device.

```python
import math
import jax
import jax.numpy as jnp
import numpy as np
from jax import lax

D = 2048
HEAD_COUNT = 16
HEAD_SIZE = 128
BLOCK = 128
DILATED_KEPT = 16
NSLIDE = 8
TOKENS = 32768
SPAN = 512
BLOCK_TOTAL = 256
MOST_SLIDE = 160
N_SEQ = 64


def paired_weights(key):
    base = jax.random.fold_in(key, 11)
    first, second = jax.random.split(base, 2)
    scale = 2.0 / math.sqrt(D)
    shape = (D, HEAD_COUNT * HEAD_SIZE)
    query = jnp.clip(jax.random.normal(first, shape, jnp.float32), -6.0, 6.0) * scale
    keyed = jnp.clip(jax.random.normal(second, shape, jnp.float32), -6.0, 6.0) * scale
    return (query, keyed)


def draw_w_query(key, part):
    return paired_weights(key)[0].astype(jnp.bfloat16)


def draw_w_key(key, part):
    return paired_weights(key)[1].astype(jnp.bfloat16)


def draw_normed(key, part):
    base = jax.random.fold_in(key, 23)
    first = jax.random.fold_in(base, 0)
    values = jnp.clip(jax.random.normal(first, (TOKENS, D), jnp.float32), -6.0, 6.0)
    return values.astype(jnp.bfloat16)


def block_scale(stream_key, dims, pieces, least, top_value):
    def one(dim, blocks):
        heights = jax.random.uniform(jax.random.fold_in(jax.random.fold_in(stream_key, 6), dim), (blocks,), jnp.float32, least / len(pieces), top_value / len(pieces))
        return jnp.repeat(jnp.exp(heights), dims[dim] // blocks).reshape((-1,) + (1,) * (len(dims) - dim - 1))

    factor_of = one(*pieces[0])
    for cut in pieces[1:]:
        factor_of = factor_of * one(*cut)
    return factor_of


def split_up(amount, total, reach, slope):
    weights = [(1 << 20) // math.isqrt(rank ** slope) + 1 for rank in range(2, amount + 1)]
    rest, counts = total - reach - (amount - 1), [1] * (amount - 1)
    while rest > 0:
        candidates = [i for i in range(amount - 1) if counts[i] < reach]
        pool, budget = sum([weights[i] for i in candidates]), rest
        for i in candidates:
            addition = min(reach - counts[i], max(1, budget * weights[i] // pool), rest)
            counts[i] = counts[i] + addition
            rest = rest - addition
    return np.array([reach] + counts)


def uneven_parts(rng, count, total, limit, lean):
    if count == 2:
        one = jax.random.randint(rng, (), max(1, total - limit), min(limit, total - 1) + 1)
        return jnp.stack([one, total - one])
    tallies = jnp.asarray(split_up(count, total, limit, lean), jnp.int32)
    twos = (count - 1) // 2
    source_of, taker = tallies[1:1 + 2 * twos:2], tallies[2:2 + 2 * twos:2]
    slack = jnp.minimum(source_of - 1, limit - taker)
    moved = jax.random.randint(jax.random.fold_in(rng, 1), (twos,), 0, 1 << 20) % (slack + 1)
    tallies = tallies.at[1:1 + 2 * twos:2].set(source_of - moved).at[2:2 + 2 * twos:2].set(taker + moved)
    return tallies[jax.random.permutation(jax.random.fold_in(rng, 2), count)]


def centred(own_key, extent, deviation, reach, cuts=(), kind=jnp.bfloat16):
    entries = deviation * jax.random.normal(own_key, extent, jnp.float32)
    if cuts:
        entries = entries * block_scale(own_key, extent, cuts, -0.22, 0.18)
    return jnp.clip(entries, -reach, reach).astype(kind)


def setup_inputs(seed: int = 0) -> dict:
    keys = jax.random.split(jax.random.key(seed), 8)
    return {
        "normed": draw_normed(jax.random.fold_in(keys[7], 71), 0),
        "w_query": draw_w_query(jax.random.fold_in(keys[7], 71), 0),
        "w_key": draw_w_key(jax.random.fold_in(keys[7], 71), 0),
        "w_value": centred(keys[3], (D, HEAD_COUNT * HEAD_SIZE), D ** -0.5, 0.125, ((1, 4),)),
        "w_out": centred(keys[4], (HEAD_COUNT * HEAD_SIZE, D), (HEAD_COUNT * HEAD_SIZE // 4) ** -0.5, 0.25, ((0, 4),)),
        "pattern": jax.vmap(lambda own: jax.random.permutation(own, BLOCK))(jax.random.split(keys[5], HEAD_COUNT)).reshape((HEAD_COUNT, BLOCK)).astype(jnp.int32),
        "slide_lengths": uneven_parts(keys[6], NSLIDE, BLOCK_TOTAL, MOST_SLIDE, 2).astype(jnp.int32),
    }


def reference(normed, w_query, w_key, w_value, w_out, pattern, slide_lengths):
    queries = jnp.dot(normed, w_query, preferred_element_type=jnp.float32).astype(jnp.bfloat16)
    keys_all = jnp.dot(normed, w_key, preferred_element_type=jnp.float32).astype(jnp.bfloat16)
    values_all = jnp.dot(normed, w_value, preferred_element_type=jnp.float32).astype(jnp.bfloat16)
    span_of_blocks = SPAN // BLOCK
    slide_ends = jnp.cumsum(slide_lengths).astype(jnp.int32)
    block_ids = jnp.arange(BLOCK_TOTAL, dtype=jnp.int32)
    slide_per_block = lax.optimization_barrier(jnp.sum((block_ids[:, None] >= slide_ends[None, :]).astype(jnp.int32), axis=1))
    kept_positions = pattern[:, :DILATED_KEPT].astype(jnp.int32)

    def dilate(source):
        by_head = jnp.moveaxis(source.reshape(BLOCK_TOTAL, BLOCK, HEAD_COUNT, HEAD_SIZE), 2, 0)
        selected_keys = jax.vmap(lambda rows, where_at: rows[:, where_at, :])(by_head, kept_positions)
        return selected_keys.reshape(HEAD_COUNT, BLOCK_TOTAL * DILATED_KEPT, HEAD_SIZE)
    far_keys = dilate(keys_all).astype(jnp.float32)
    far_values = dilate(values_all).astype(jnp.float32)
    distant_block = jnp.arange(BLOCK_TOTAL * DILATED_KEPT, dtype=jnp.int32) // DILATED_KEPT
    distant_slide = jnp.repeat(slide_per_block, DILATED_KEPT)
    far_span = distant_block // span_of_blocks
    row_slide = jnp.repeat(slide_per_block, BLOCK).reshape(N_SEQ, SPAN)

    def by_span(source):
        return jnp.transpose(source.reshape(N_SEQ, SPAN, HEAD_COUNT, HEAD_SIZE), (0, 2, 1, 3))
    scale = 1.0 / math.sqrt(HEAD_SIZE)

    def one_span(item):
        query_s, key_s, value_s, slide_s, span_id = item
        query_f = query_s.astype(jnp.float32)
        near = jnp.einsum('hqd,hkd->hqk', query_f, key_s.astype(jnp.float32)) * scale
        far = jnp.einsum('hqd,hkd->hqk', query_f, far_keys) * scale
        near_mask = slide_s[:, None] == slide_s[None, :]
        far_mask = (slide_s[:, None] == distant_slide[None, :]) & (far_span != span_id)[None, :]
        near = jnp.where(near_mask[None], near, -1e+30)
        far = jnp.where(far_mask[None], far, -1e+30)
        peak = jnp.maximum(lax.optimization_barrier(jnp.max(near, axis=2, keepdims=True)), lax.optimization_barrier(jnp.max(far, axis=2, keepdims=True)))
        near_exp = jnp.exp(near - peak)
        far_exp = jnp.exp(far - peak)
        total = lax.optimization_barrier(jnp.sum(near_exp, axis=2, keepdims=True)) + lax.optimization_barrier(jnp.sum(far_exp, axis=2, keepdims=True))
        near_w = (near_exp / total).astype(jnp.bfloat16).astype(jnp.float32)
        far_w = (far_exp / total).astype(jnp.bfloat16).astype(jnp.float32)
        context = jnp.einsum('hqk,hkd->hqd', near_w, value_s.astype(jnp.float32))
        context = context + jnp.einsum('hqk,hkd->hqd', far_w, far_values)
        return jnp.transpose(context.astype(jnp.bfloat16), (1, 0, 2)).reshape(SPAN, HEAD_COUNT * HEAD_SIZE)
    span_ids = jnp.arange(N_SEQ, dtype=jnp.int32)
    context = lax.map(one_span, (by_span(queries), by_span(keys_all), by_span(values_all), row_slide, span_ids))
    context = context.reshape(TOKENS, HEAD_COUNT * HEAD_SIZE)
    return jnp.dot(context, w_out, preferred_element_type=jnp.float32).astype(jnp.bfloat16)
```

```python
import functools
import math

import jax
import jax.numpy as jnp
from jax import lax
from jax.experimental import pallas as pl
from jax.experimental.pallas import tpu as pltpu
from jax.sharding import PartitionSpec as P

HEAD = 128
BLOCK = 128
KEPT = 16
MESH = pl.DeviceIdType.MESH
NX, NY, NZ = 2, 4, 8
SPANS = NX * NY * NZ
ROW_CUTS = 4
FAR_STEP = 8
LOG2E = 1.4426950408889634


def position():
    seq = lax.axis_index("seq")
    sub = lax.axis_index("sub")
    x = seq // (NY * NZ)
    y = (seq // NZ) % NY
    z = seq % NZ
    return seq, sub, x, y, z


def span_at(x, y, z):
    return x * (NY * NZ) + y * NZ + z


def remote(src, dst, send, recv, seq, sub):
    return pltpu.make_async_remote_copy(
        src_ref=src,
        dst_ref=dst,
        send_sem=send,
        recv_sem=recv,
        device_id=(seq, sub),
        device_id_type=MESH,
    )


def greet(places):
    barrier = pltpu.get_barrier_semaphore()
    for seq, sub in places:
        pl.semaphore_signal(barrier, inc=1, device_id=(seq, sub), device_id_type=MESH)
    pl.semaphore_wait(barrier, len(places))


def exchange_kernel(
    x_hbm, wq_hbm, wk_hbm, wv_hbm, pat_ref, far_ref, group_ref,
    xs, ws, qkv, dil,
    local_sem, w_sem, own_sem,
    mate_send, mate_recv, cross_send, cross_recv, pass_send, pass_recv,
    dil_send, group_send, group_recv, far_recv, x_send, z_send,
):
    seq, sub, x, y, z = position()
    core = sub % 2
    chip = sub // 2
    mate = sub + 1 - 2 * core
    over = (sub + 2) % 4
    rows = xs.shape[1]
    cut = rows // ROW_CUTS

    own_x = pltpu.make_async_copy(x_hbm, xs.at[sub], local_sem)
    own_x.start()
    weights = []
    for index, (source, half) in enumerate(
        [(wk_hbm, 0), (wk_hbm, 1), (wv_hbm, 0), (wv_hbm, 1), (wq_hbm, 0), (wq_hbm, 1)]
    ):
        copy = pltpu.make_async_copy(
            source.at[:, half * 256 : (half + 1) * 256], ws.at[index], w_sem.at[index]
        )
        copy.start()
        weights.append(copy)

    side = span_at(1 - x, y, z)
    above = span_at(x, y, (z + 1) % NZ)
    below = span_at(x, y, (z + NZ - 1) % NZ)
    fellows = [span_at(x, (y + dy) % NY, z) for dy in (1, 2, 3)]
    greet(
        [(seq, mate), (seq, over), (side, sub), (above, sub), (below, sub)]
        + [(fellow, sub) for fellow in fellows]
    )

    crossing = []
    for r in range(ROW_CUTS):
        part = slice(r * cut, (r + 1) * cut)
        copy = remote(
            x_hbm.at[part], xs.at[sub, part], cross_send.at[r], cross_recv.at[r], seq, over
        )
        copy.start()
        crossing.append(copy)
    to_mate = remote(x_hbm, xs.at[sub], mate_send, mate_recv, seq, mate)
    to_mate.start()

    def project(which):
        lhs = xs[pl.ds(2 * which, 2)].reshape(2 * rows, xs.shape[2])
        top = pl.multiple_of(which * (2 * rows), 2 * rows)
        for index in range(6):
            out = jnp.dot(lhs, ws[index], preferred_element_type=jnp.float32)
            out = out.astype(jnp.bfloat16)
            kind = (1, 2, 0)[index // 2]
            first = 2 * (index % 2)
            qkv[first, kind, pl.ds(top, 2 * rows), :] = out[:, :HEAD]
            qkv[first + 1, kind, pl.ds(top, 2 * rows), :] = out[:, HEAD:]

    own_x.wait()
    to_mate.wait_recv()
    for copy in weights:
        copy.wait()
    project(chip)

    passing = []
    for r in range(ROW_CUTS):
        part = slice(r * cut, (r + 1) * cut)
        crossing[r].wait_recv()
        copy = remote(
            xs.at[over, part], xs.at[over, part], pass_send.at[r], pass_recv.at[r], seq, mate
        )
        copy.start()
        passing.append(copy)
    for copy in passing:
        copy.wait_recv()
    project(1 - chip)

    blocks = qkv.shape[2] // BLOCK
    half = blocks * KEPT
    line = lax.broadcasted_iota(jnp.int32, (BLOCK, BLOCK), 0)
    for head in range(NY):
        hit = (line == pat_ref[head : head + 1, :]).astype(jnp.float32)
        pick = hit.T[:KEPT, :].astype(jnp.bfloat16)
        for kind in (1, 2):
            for b in range(blocks):
                taken = jnp.dot(
                    pick,
                    qkv[head, kind, b * BLOCK : (b + 1) * BLOCK, :],
                    preferred_element_type=jnp.float32,
                )
                base = (kind - 1) * half + b * KEPT
                dil[head, base : base + KEPT, :] = taken.astype(jnp.bfloat16)

    own_far = pltpu.make_async_copy(dil.at[y], far_ref.at[seq], own_sem.at[0])
    own_far.start()
    sent = []
    for dy in (1, 3, 2):
        head = (y + dy) % NY
        copy = remote(
            dil.at[head], far_ref.at[seq], dil_send.at[dy], far_recv.at[seq],
            span_at(x, head, z), sub,
        )
        copy.start()
        sent.append(copy)
    own_group = pltpu.make_async_copy(qkv.at[y], group_ref.at[y], own_sem.at[1])
    own_group.start()
    for dy in (1, 3, 2):
        head = (y + dy) % NY
        copy = remote(
            qkv.at[head], group_ref.at[y], group_send.at[dy], group_recv.at[y],
            span_at(x, head, z), sub,
        )
        copy.start()
        sent.append(copy)

    x_count = [0]
    z_count = [0]

    def arrived(slot):
        remote(far_ref.at[slot], far_ref.at[slot], x_send.at[0], far_recv.at[slot], side, sub).wait_recv()

    def put(slot, place, sems, count):
        copy = remote(
            far_ref.at[slot], far_ref.at[slot], sems.at[count[0]], far_recv.at[slot], place, sub
        )
        count[0] += 1
        copy.start()
        sent.append(copy)

    order = (0, 1, 3, 2)
    early = (0, 1)
    for dy in order:
        slot = span_at(x, (y + dy) % NY, z)
        if dy == 0:
            own_far.wait()
        else:
            arrived(slot)
        put(slot, side, x_send, x_count)
        put(slot, above, z_send, z_count)
        put(slot, below, z_send, z_count)
    for dy in early:
        slot = span_at(1 - x, (y + dy) % NY, z)
        arrived(slot)
        put(slot, above, z_send, z_count)
        put(slot, below, z_send, z_count)
    half_up = {(0, 0), (0, 3), (1, 0)}
    for d in range(1, 5):
        for part in [(0, dy) for dy in order] + [(1, dy) for dy in early]:
            other, dy = part
            for up in (True, False):
                if d == 4 and up != (part in half_up):
                    continue
                source = (z + NZ - d) % NZ if up else (z + d) % NZ
                slot = span_at((x + other) % NX, (y + dy) % NY, source)
                arrived(slot)
                if d < 3 or (d == 3 and up == (part in half_up)):
                    put(slot, above if up else below, z_send, z_count)
                if other == 0 and dy not in early:
                    put(slot, side, x_send, x_count)
    for dy in order:
        if dy in early:
            continue
        for d in range(NZ):
            arrived(span_at(1 - x, (y + dy) % NY, (z + d) % NZ))

    own_group.wait()
    for dy in (1, 2, 3):
        fellow = (y + dy) % NY
        remote(
            qkv.at[fellow], group_ref.at[fellow], group_send.at[dy], group_recv.at[fellow],
            span_at(x, fellow, z), sub,
        ).wait_recv()
    for copy in crossing + [to_mate] + passing + sent:
        copy.wait_send()


def exchange(normed, w_query, w_key, w_value, pattern):
    rows, width = normed.shape
    span = 4 * rows
    kept = 2 * (span // BLOCK) * KEPT
    any_spec = pl.BlockSpec(memory_space=pl.ANY)
    vmem_spec = pl.BlockSpec(memory_space=pltpu.VMEM)
    dma = pltpu.SemaphoreType.DMA
    return pl.pallas_call(
        exchange_kernel,
        out_shape=(
            jax.ShapeDtypeStruct((SPANS, kept, HEAD), jnp.bfloat16),
            jax.ShapeDtypeStruct((NY, 3, span, HEAD), jnp.bfloat16),
        ),
        in_specs=[any_spec] * 4 + [vmem_spec],
        out_specs=(vmem_spec, vmem_spec),
        scratch_shapes=[
            pltpu.VMEM((4, rows, width), jnp.bfloat16),
            pltpu.VMEM((6, width, 256), jnp.bfloat16),
            pltpu.VMEM((NY, 3, span, HEAD), jnp.bfloat16),
            pltpu.VMEM((NY, kept, HEAD), jnp.bfloat16),
            dma, dma((6,)), dma((2,)),
            dma, dma, dma((ROW_CUTS,)), dma((ROW_CUTS,)), dma((ROW_CUTS,)), dma((ROW_CUTS,)),
            dma((NY,)), dma((NY,)), dma((NY,)), dma((SPANS,)), dma((20,)), dma((44,)),
        ],
        compiler_params=pltpu.CompilerParams(
            collective_id=0, has_side_effects=True, vmem_limit_bytes=48 * 1024 * 1024
        ),
        name="exchange",
    )(normed, w_query, w_key, w_value, pattern)


def attend_kernel(slide_ref, first_ref, last_ref, far_ref, group_ref, near_ref, dist_ref, out_ref, acc, peak):
    seq, sub, x, y, z = position()
    span = group_ref.shape[2]
    blocks = span // BLOCK
    step_keys = FAR_STEP * 64
    factor = LOG2E / math.sqrt(HEAD)
    ones = jnp.ones((span, HEAD), jnp.bfloat16)

    def scores(query, keys):
        return lax.dot_general(
            query, keys, (((1,), (1,)), ((), ())), preferred_element_type=jnp.float32
        ) * factor

    def one_span(item, carry):
        mine = span_at(x, item, z)
        query = group_ref[item, 0]
        ids = [slide_ref[mine * blocks + b] for b in range(blocks)]
        tags = near_ref[pl.ds(mine, 1), :]
        seen = scores(query, group_ref[item, 1])
        bias = jnp.concatenate(
            [
                jnp.broadcast_to(jnp.where(tags == ids[b], 0.0, -1e30), (BLOCK, span))
                for b in range(blocks)
            ],
            axis=0,
        )
        seen = seen + bias
        top = jnp.max(seen, axis=1, keepdims=True)
        weight = jnp.exp2(seen - top).astype(jnp.bfloat16)
        extended = jnp.concatenate([group_ref[item, 2], ones], axis=1)
        acc[...] = jnp.dot(weight, extended, preferred_element_type=jnp.float32)
        peak[...] = jnp.broadcast_to(top, peak.shape)

        def far_step(index, inner):
            base = index * FAR_STEP
            part = far_ref[pl.ds(base, FAR_STEP)]
            keys = part[:, :64, :].reshape(step_keys, HEAD)
            values = part[:, 64:, :].reshape(step_keys, HEAD)
            label = dist_ref[pl.ds(index, 1), :]
            where = base + lax.broadcasted_iota(jnp.int32, (1, step_keys), 1) // 64
            label = jnp.where(where == mine, -1, label)
            got = scores(query, keys)
            bias = jnp.concatenate(
                [
                    jnp.broadcast_to(jnp.where(label == ids[b], 0.0, -1e30), (BLOCK, step_keys))
                    for b in range(blocks)
                ],
                axis=0,
            )
            got = got + bias
            old = peak[:, :1]
            new = jnp.maximum(old, jnp.max(got, axis=1, keepdims=True))
            weight = jnp.exp2(got - new).astype(jnp.bfloat16)
            wide = jnp.concatenate([values, ones], axis=1)
            acc[...] = acc[...] * jnp.exp2(old - new) + jnp.dot(
                weight, wide, preferred_element_type=jnp.float32
            )
            peak[...] = jnp.broadcast_to(new, peak.shape)
            return inner

        low = first_ref[ids[0]] // (blocks * FAR_STEP)
        high = (last_ref[ids[blocks - 1]] + blocks * FAR_STEP - 1) // (blocks * FAR_STEP)
        lax.fori_loop(low, high, far_step, 0)
        out_ref[item] = (acc[:, :HEAD] / acc[:, HEAD:]).astype(jnp.bfloat16)
        return carry

    lax.fori_loop(0, NY, one_span, 0)


def attend(far, group, slide_lengths):
    span = group.shape[2]
    blocks = span // BLOCK
    total = SPANS * blocks
    ends = jnp.cumsum(slide_lengths)
    starts = ends - slide_lengths
    index = jnp.arange(total, dtype=jnp.int32)
    slide = jnp.sum((index[:, None] >= ends[None, :]).astype(jnp.int32), axis=1)
    near = jnp.repeat(slide, BLOCK).reshape(SPANS, span)
    dist = jnp.repeat(slide, KEPT).reshape(SPANS // FAR_STEP, FAR_STEP * blocks * KEPT)
    smem = pl.BlockSpec(memory_space=pltpu.SMEM)
    vmem = pl.BlockSpec(memory_space=pltpu.VMEM)
    return pl.pallas_call(
        attend_kernel,
        out_shape=jax.ShapeDtypeStruct((NY, span, HEAD), jnp.bfloat16),
        in_specs=[smem] * 3 + [vmem] * 4,
        out_specs=vmem,
        scratch_shapes=[
            pltpu.VMEM((span, 2 * HEAD), jnp.float32),
            pltpu.VMEM((span, HEAD), jnp.float32),
        ],
        compiler_params=pltpu.CompilerParams(vmem_limit_bytes=48 * 1024 * 1024),
        name="attend",
    )(slide, starts, ends, far, group, near, dist)


def merge_kernel(
    ctx_ref, wo_hbm, out_ref,
    ctx, wo, away, home, give_mate, give_over, give_home, take_mate, take_over, take_home,
    w_sem, own_sem, ctx_send, ctx_recv,
    mate_send, mate_recv, over_send, over_recv, home_send, home_recv,
):
    seq, sub, x, y, z = position()
    core = sub % 2
    chip = sub // 2
    mate = sub + 1 - 2 * core
    over = (sub + 2) % 4
    pieces = away.shape[0]
    cols = away.shape[3]
    rows = away.shape[2]
    load = pltpu.make_async_copy(wo_hbm, wo, w_sem)
    load.start()
    fellows = [span_at(x, (y + dy) % NY, z) for dy in (1, 2, 3)]
    greet([(seq, mate), (seq, over)] + [(fellow, sub) for fellow in fellows])

    lane = pl.ds(pl.multiple_of(y * HEAD, HEAD), HEAD)
    own = pltpu.make_async_copy(ctx_ref.at[y], ctx.at[:, lane], own_sem)
    own.start()
    sent = []
    incoming = []
    for part in (0, 1):
        which = 1 - chip if part == 0 else chip
        lines = pl.ds(pl.multiple_of(which * 2 * rows, 2 * rows), 2 * rows)
        group = []
        for dy in (1, 3, 2):
            to = (y + dy) % NY
            copy = remote(
                ctx_ref.at[to, lines], ctx.at[lines, lane],
                ctx_send.at[part, dy], ctx_recv.at[part, dy], span_at(x, to, z), sub,
            )
            copy.start()
            group.append(copy)
        sent += group
        incoming.append(group)
    own.wait()
    load.wait()
    for copy in incoming[0]:
        copy.wait_recv()

    def product(which, piece):
        lines = pl.ds(pl.multiple_of(which * 2 * rows, 2 * rows), 2 * rows)
        return jnp.dot(
            ctx[lines, :], wo[:, piece * cols : (piece + 1) * cols],
            preferred_element_type=jnp.float32,
        ).reshape(2, rows, cols)

    to_mate = []
    to_over = []

    def forward(piece):
        to_mate[piece].wait_recv()
        total = away[piece, core] + take_mate[piece].astype(jnp.float32)
        give_over[piece] = total.astype(jnp.bfloat16)
        copy = remote(
            give_over.at[piece], take_over.at[piece],
            over_send.at[piece], over_recv.at[piece], seq, over,
        )
        copy.start()
        to_over.append(copy)

    for piece in range(pieces):
        away[piece] = product(1 - chip, piece)
        give_mate[piece] = away[piece, 1 - core].astype(jnp.bfloat16)
        copy = remote(
            give_mate.at[piece], take_mate.at[piece],
            mate_send.at[piece], mate_recv.at[piece], seq, mate,
        )
        copy.start()
        to_mate.append(copy)
        if piece:
            forward(piece - 1)
    forward(pieces - 1)

    for copy in incoming[1]:
        copy.wait_recv()
    to_home = []
    for piece in range(pieces):
        home[piece] = product(chip, piece)
        give_home[piece] = home[piece, 1 - core].astype(jnp.bfloat16)
        copy = remote(
            give_home.at[piece], take_home.at[piece],
            home_send.at[piece], home_recv.at[piece], seq, mate,
        )
        copy.start()
        to_home.append(copy)
    for piece in range(pieces):
        to_home[piece].wait_recv()
        to_over[piece].wait_recv()
        total = home[piece, core] + take_home[piece].astype(jnp.float32)
        total = total + take_over[piece].astype(jnp.float32)
        out_ref[:, piece * cols : (piece + 1) * cols] = total.astype(jnp.bfloat16)
    for copy in sent + to_mate + to_over + to_home:
        copy.wait_send()


def merge(ctx, w_out):
    span = ctx.shape[1]
    rows = span // 4
    depth, width = w_out.shape
    pieces = 4
    cols = width // pieces
    dma = pltpu.SemaphoreType.DMA
    half = pltpu.VMEM((pieces, rows, cols), jnp.bfloat16)
    return pl.pallas_call(
        merge_kernel,
        out_shape=jax.ShapeDtypeStruct((rows, width), jnp.bfloat16),
        in_specs=[
            pl.BlockSpec(memory_space=pltpu.VMEM),
            pl.BlockSpec(memory_space=pl.ANY),
        ],
        out_specs=pl.BlockSpec(memory_space=pltpu.VMEM),
        scratch_shapes=[
            pltpu.VMEM((span, depth), jnp.bfloat16),
            pltpu.VMEM((depth, width), jnp.bfloat16),
            pltpu.VMEM((pieces, 2, rows, cols), jnp.float32),
            pltpu.VMEM((pieces, 2, rows, cols), jnp.float32),
            half, half, half, half, half, half,
            dma, dma, dma((2, NY)), dma((2, NY)),
            dma((pieces,)), dma((pieces,)), dma((pieces,)), dma((pieces,)),
            dma((pieces,)), dma((pieces,)),
        ],
        compiler_params=pltpu.CompilerParams(
            collective_id=1, has_side_effects=True, vmem_limit_bytes=48 * 1024 * 1024
        ),
        name="merge",
    )(ctx, w_out)


def shards(normed, w_query, w_key, w_value, w_out, pattern, slide_lengths):
    far, group = exchange(normed, w_query, w_key, w_value, pattern)
    ctx = attend(far, group, slide_lengths)
    return merge(ctx, w_out)


def solution(mesh):
    placed = (
        P(("seq", "sub"), None),
        P(None, "sub"),
        P(None, "sub"),
        P(None, "sub"),
        P("sub", None),
        P("sub", None),
        P(),
    )
    return jax.shard_map(
        shards, mesh=mesh, in_specs=placed, out_specs=P(("seq", "sub"), None), check_vma=False
    )
```

```python
import functools
import math

import jax
import jax.numpy as jnp
from jax import lax
from jax.experimental import pallas as pl
from jax.experimental.pallas import tpu as pltpu
from jax.sharding import PartitionSpec as P

HEAD = 128
BLOCK = 128
KEPT = 16
MESH = pl.DeviceIdType.MESH
NX, NY, NZ = 2, 4, 8
SPANS = NX * NY * NZ
ROW_CUTS = 8
FAR_STEP = 8
LOG2E = 1.4426950408889634
NSLIDE = 8
HIDE = -1e30


def position():
    seq = lax.axis_index("seq")
    sub = lax.axis_index("sub")
    x = seq // (NY * NZ)
    y = (seq // NZ) % NY
    z = seq % NZ
    return seq, sub, x, y, z


def span_at(x, y, z):
    return x * (NY * NZ) + y * NZ + z


def remote(src, dst, send, recv, seq, sub):
    return pltpu.make_async_remote_copy(
        src_ref=src,
        dst_ref=dst,
        send_sem=send,
        recv_sem=recv,
        device_id=(seq, sub),
        device_id_type=MESH,
    )


def greet(places):
    barrier = pltpu.get_barrier_semaphore()
    for seq, sub in places:
        pl.semaphore_signal(barrier, inc=1, device_id=(seq, sub), device_id_type=MESH)
    pl.semaphore_wait(barrier, len(places))


def exchange_kernel(
    x_hbm, wq_hbm, wk_hbm, wv_hbm, pat_ref, far_ref, group_ref,
    xs, ws, relay, qkv, dil,
    local_sem, w_sem, own_sem,
    mate_send, mate_recv, out_send, out_recv, cross_send, cross_recv, pass_send, pass_recv,
    dil_send, group_send, group_recv, far_recv, x_send, z_send,
):
    seq, sub, x, y, z = position()
    core = sub % 2
    chip = sub // 2
    mate = sub + 1 - 2 * core
    over = (sub + 2) % 4
    rows = xs.shape[1]
    cut = rows // ROW_CUTS

    own_x = pltpu.make_async_copy(x_hbm, xs.at[sub], local_sem)
    own_x.start()
    weights = []
    for index, (source, half) in enumerate(
        [(wk_hbm, 0), (wk_hbm, 1), (wv_hbm, 0), (wv_hbm, 1), (wq_hbm, 0), (wq_hbm, 1)]
    ):
        copy = pltpu.make_async_copy(
            source.at[:, half * 256 : (half + 1) * 256], ws.at[index], w_sem.at[index]
        )
        copy.start()
        weights.append(copy)

    side = span_at(1 - x, y, z)
    above = span_at(x, y, (z + 1) % NZ)
    below = span_at(x, y, (z + NZ - 1) % NZ)
    fellows = [span_at(x, (y + dy) % NY, z) for dy in (1, 2, 3)]
    greet(
        [(seq, mate), (side, sub), (side, over), (above, sub), (below, sub)]
        + [(fellow, sub) for fellow in fellows]
    )

    outgoing = []
    for r in range(ROW_CUTS):
        part = slice(r * cut, (r + 1) * cut)
        copy = remote(
            x_hbm.at[part], relay.at[r], out_send.at[r], out_recv.at[r],
            side, over if r % 2 else sub,
        )
        copy.start()
        outgoing.append(copy)
    to_mate = remote(x_hbm, xs.at[sub], mate_send, mate_recv, seq, mate)
    to_mate.start()
    crossing = []

    def carry_on(r):
        part = slice(r * cut, (r + 1) * cut)
        outgoing[r].wait_recv()
        copy = remote(
            relay.at[r], xs.at[over if r % 2 else sub, part], cross_send.at[r], cross_recv.at[r],
            side, sub if r % 2 else over,
        )
        copy.start()
        crossing.append(copy)

    def project(which, indices):
        lhs = xs[pl.ds(2 * which, 2)].reshape(2 * rows, xs.shape[2])
        top = pl.multiple_of(which * (2 * rows), 2 * rows)
        for index in indices:
            out = jnp.dot(lhs, ws[index], preferred_element_type=jnp.float32)
            out = out.astype(jnp.bfloat16)
            kind = (1, 2, 0)[index // 2]
            first = 2 * (index % 2)
            qkv[first, kind, pl.ds(top, 2 * rows), :] = out[:, :HEAD]
            qkv[first + 1, kind, pl.ds(top, 2 * rows), :] = out[:, HEAD:]

    own_x.wait()
    to_mate.wait_recv()
    for third in range(3):
        weights[2 * third].wait()
        weights[2 * third + 1].wait()
        project(chip, (2 * third, 2 * third + 1))
        for r in range(2 * third, 2 * third + 2):
            carry_on(r)
    for r in range(6, ROW_CUTS):
        carry_on(r)

    passing = []
    for r in range(ROW_CUTS):
        part = slice(r * cut, (r + 1) * cut)
        remote(
            relay.at[r], xs.at[over, part], cross_send.at[r], cross_recv.at[r], side, sub
        ).wait_recv()
        copy = remote(
            xs.at[over, part], xs.at[over, part], pass_send.at[r], pass_recv.at[r], seq, mate
        )
        copy.start()
        passing.append(copy)
    for copy in passing:
        copy.wait_recv()
    project(1 - chip, range(6))

    blocks = qkv.shape[2] // BLOCK
    half = blocks * KEPT
    line = lax.broadcasted_iota(jnp.int32, (BLOCK, BLOCK), 0)
    for head in range(NY):
        hit = (line == pat_ref[head : head + 1, :]).astype(jnp.float32)
        pick = hit.T[:KEPT, :].astype(jnp.bfloat16)
        for kind in (1, 2):
            for b in range(blocks):
                taken = jnp.dot(
                    pick,
                    qkv[head, kind, b * BLOCK : (b + 1) * BLOCK, :],
                    preferred_element_type=jnp.float32,
                )
                base = (kind - 1) * half + b * KEPT
                dil[head, base : base + KEPT, :] = taken.astype(jnp.bfloat16)

    own_far = pltpu.make_async_copy(dil.at[y], far_ref.at[seq], own_sem.at[0])
    own_far.start()
    sent = []
    for dy in (1, 3, 2):
        head = (y + dy) % NY
        copy = remote(
            dil.at[head], far_ref.at[seq], dil_send.at[dy], far_recv.at[seq],
            span_at(x, head, z), sub,
        )
        copy.start()
        sent.append(copy)
    own_group = pltpu.make_async_copy(qkv.at[y], group_ref.at[y], own_sem.at[1])
    own_group.start()
    for dy in (1, 3, 2):
        head = (y + dy) % NY
        copy = remote(
            qkv.at[head], group_ref.at[y], group_send.at[dy], group_recv.at[y],
            span_at(x, head, z), sub,
        )
        copy.start()
        sent.append(copy)

    x_count = [0]
    z_count = [0]

    def arrived(slot):
        remote(far_ref.at[slot], far_ref.at[slot], x_send.at[0], far_recv.at[slot], side, sub).wait_recv()

    def put(slot, place, sems, count):
        copy = remote(
            far_ref.at[slot], far_ref.at[slot], sems.at[count[0]], far_recv.at[slot], place, sub
        )
        count[0] += 1
        copy.start()
        sent.append(copy)

    order = (0, 1, 3, 2)
    early = (0, 1)
    for dy in order:
        slot = span_at(x, (y + dy) % NY, z)
        if dy == 0:
            own_far.wait()
        else:
            arrived(slot)
        put(slot, side, x_send, x_count)
        put(slot, above, z_send, z_count)
        put(slot, below, z_send, z_count)
    for dy in early:
        slot = span_at(1 - x, (y + dy) % NY, z)
        arrived(slot)
        put(slot, above, z_send, z_count)
        put(slot, below, z_send, z_count)
    half_up = {(0, 0), (0, 3), (1, 0)}
    for d in range(1, 5):
        for part in [(0, dy) for dy in order] + [(1, dy) for dy in early]:
            other, dy = part
            for up in (True, False):
                if d == 4 and up != (part in half_up):
                    continue
                source = (z + NZ - d) % NZ if up else (z + d) % NZ
                slot = span_at((x + other) % NX, (y + dy) % NY, source)
                arrived(slot)
                if d < 3 or (d == 3 and up == (part in half_up)):
                    put(slot, above if up else below, z_send, z_count)
                if other == 0 and dy not in early:
                    put(slot, side, x_send, x_count)
    for dy in order:
        if dy in early:
            continue
        for d in range(NZ):
            arrived(span_at(1 - x, (y + dy) % NY, (z + d) % NZ))

    own_group.wait()
    for dy in (1, 2, 3):
        fellow = (y + dy) % NY
        remote(
            qkv.at[fellow], group_ref.at[fellow], group_send.at[dy], group_recv.at[fellow],
            span_at(x, fellow, z), sub,
        ).wait_recv()
    for copy in outgoing + crossing + [to_mate] + passing + sent:
        copy.wait_send()


def exchange(normed, w_query, w_key, w_value, pattern):
    rows, width = normed.shape
    span = 4 * rows
    kept = 2 * (span // BLOCK) * KEPT
    any_spec = pl.BlockSpec(memory_space=pl.ANY)
    vmem_spec = pl.BlockSpec(memory_space=pltpu.VMEM)
    dma = pltpu.SemaphoreType.DMA
    return pl.pallas_call(
        exchange_kernel,
        out_shape=(
            jax.ShapeDtypeStruct((SPANS, kept, HEAD), jnp.bfloat16),
            jax.ShapeDtypeStruct((NY, 3, span, HEAD), jnp.bfloat16),
        ),
        in_specs=[any_spec] * 4 + [vmem_spec],
        out_specs=(vmem_spec, vmem_spec),
        scratch_shapes=[
            pltpu.VMEM((4, rows, width), jnp.bfloat16),
            pltpu.VMEM((6, width, 256), jnp.bfloat16),
            pltpu.VMEM((ROW_CUTS, rows // ROW_CUTS, width), jnp.bfloat16),
            pltpu.VMEM((NY, 3, span, HEAD), jnp.bfloat16),
            pltpu.VMEM((NY, kept, HEAD), jnp.bfloat16),
            dma, dma((6,)), dma((2,)),
            dma, dma, dma((ROW_CUTS,)), dma((ROW_CUTS,)), dma((ROW_CUTS,)), dma((ROW_CUTS,)),
            dma((ROW_CUTS,)), dma((ROW_CUTS,)),
            dma((NY,)), dma((NY,)), dma((NY,)), dma((SPANS,)), dma((20,)), dma((44,)),
        ],
        compiler_params=pltpu.CompilerParams(
            collective_id=0, has_side_effects=True, vmem_limit_bytes=48 * 1024 * 1024
        ),
        name="exchange",
    )(normed, w_query, w_key, w_value, pattern)


def attend_kernel(len_ref, far_ref, group_ref, out_ref, key_mark, turned, query, acc, peak):
    seq, sub, x, y, z = position()
    span = group_ref.shape[2]
    blocks = span // BLOCK
    keys_step = FAR_STEP * blocks * KEPT
    factor = LOG2E / math.sqrt(HEAD)
    col = lax.broadcasted_iota(jnp.int32, (1, HEAD), 1)
    low = (col - NSLIDE) * blocks
    high = low + blocks
    starts, ends = [], []
    total = jnp.int32(0)
    for j in range(NSLIDE):
        starts.append(total)
        total = total + len_ref[j]
        ends.append(total)
        low = jnp.where(col == j, starts[j], low)
        high = jnp.where(col == j, ends[j], high)
    flag = jnp.where(col < NSLIDE, 1.0, 0.0)

    def inside(first, count, size):
        block = first + lax.broadcasted_iota(jnp.int32, (count, HEAD), 0) // size
        return jnp.where((block >= low) & (block < high), 1.0, 0.0)

    for i in range(SPANS // FAR_STEP):
        got = inside(i * FAR_STEP * blocks, keys_step, KEPT)
        key_mark[i] = (HIDE * jnp.abs(got - flag)).astype(jnp.bfloat16)
        values = far_ref[i * FAR_STEP : (i + 1) * FAR_STEP, blocks * KEPT :, :]
        turned[i, :HEAD, :] = values.reshape(keys_step, HEAD).T
        turned[i, HEAD:, :] = jnp.ones((16, keys_step), jnp.bfloat16)

    def one_span(item, carry):
        mine = span_at(x, item, z)
        first = mine * blocks
        got = inside(first, span, BLOCK)
        mark = flag * got + jnp.where(col == NSLIDE + mine, 1.0, 0.0)
        query[:HEAD, :] = group_ref[item, 0].T
        query[HEAD:, :] = mark.astype(jnp.bfloat16).T
        near_mark = (HIDE * (flag * (1.0 - got))).astype(jnp.bfloat16)

        def update(keys, values, begin):
            got = jnp.dot(keys, query[...], preferred_element_type=jnp.float32)
            top = jnp.max(got, axis=0, keepdims=True)
            if not begin:
                old = peak[:1, :]
                top = jnp.maximum(old, top)
            weight = jnp.exp2(got * factor - top * factor).astype(jnp.bfloat16)
            out = jnp.dot(values, weight, preferred_element_type=jnp.float32)
            if not begin:
                out = out + acc[...] * jnp.exp2((old - top) * factor)
            acc[...] = out
            peak[...] = jnp.broadcast_to(top, peak.shape)

        values = jnp.concatenate(
            [group_ref[item, 2].T, jnp.ones((16, span), jnp.bfloat16)], axis=0
        )
        update(jnp.concatenate([group_ref[item, 1], near_mark], axis=1), values, True)
        begin = jnp.int32(0)
        stop = jnp.int32(SPANS * blocks)
        for j in range(NSLIDE):
            begin = jnp.where(starts[j] <= first, starts[j], begin)
            last = NSLIDE - 1 - j
            stop = jnp.where(ends[last] >= first + blocks, ends[last], stop)

        def far_step(i, inner):
            keys = far_ref[pl.ds(i * FAR_STEP, FAR_STEP), : blocks * KEPT, :]
            keys = keys.reshape(keys_step, HEAD)
            update(jnp.concatenate([keys, key_mark[i]], axis=1), turned[i], False)
            return inner

        wide = blocks * FAR_STEP
        lax.fori_loop(begin // wide, (stop + wide - 1) // wide, far_step, 0)
        out_ref[item] = (acc[:HEAD, :] / acc[HEAD : HEAD + 1, :]).T.astype(jnp.bfloat16)
        return carry

    lax.fori_loop(0, NY, one_span, 0)


def attend(far, group, slide_lengths):
    span = group.shape[2]
    keys_step = FAR_STEP * (span // BLOCK) * KEPT
    smem = pl.BlockSpec(memory_space=pltpu.SMEM)
    vmem = pl.BlockSpec(memory_space=pltpu.VMEM)
    return pl.pallas_call(
        attend_kernel,
        out_shape=jax.ShapeDtypeStruct((NY, span, HEAD), jnp.bfloat16),
        in_specs=[smem, vmem, vmem],
        out_specs=vmem,
        scratch_shapes=[
            pltpu.VMEM((SPANS // FAR_STEP, keys_step, HEAD), jnp.bfloat16),
            pltpu.VMEM((SPANS // FAR_STEP, HEAD + 16, keys_step), jnp.bfloat16),
            pltpu.VMEM((2 * HEAD, span), jnp.bfloat16),
            pltpu.VMEM((HEAD + 16, span), jnp.float32),
            pltpu.VMEM((8, span), jnp.float32),
        ],
        compiler_params=pltpu.CompilerParams(vmem_limit_bytes=48 * 1024 * 1024),
        name="attend",
    )(slide_lengths, far, group)


def merge_kernel(
    ctx_ref, wo_hbm, out_ref,
    ctx, wo, away, home, give_mate, give_over, give_home, take_mate, take_over, take_home, relay,
    w_sem, own_sem, ctx_send, ctx_recv,
    mate_send, mate_recv, over_send, over_recv, home_send, home_recv, relay_send, relay_recv,
):
    seq, sub, x, y, z = position()
    core = sub % 2
    chip = sub // 2
    mate = sub + 1 - 2 * core
    over = (sub + 2) % 4
    pieces = away.shape[0]
    cols = away.shape[3]
    rows = away.shape[2]
    load = pltpu.make_async_copy(wo_hbm, wo, w_sem)
    load.start()
    fellows = [span_at(x, (y + dy) % NY, z) for dy in (1, 2, 3)]
    side = span_at(1 - x, y, z)
    greet([(seq, mate), (side, sub), (side, over)] + [(fellow, sub) for fellow in fellows])

    lane = pl.ds(pl.multiple_of(y * HEAD, HEAD), HEAD)
    own = pltpu.make_async_copy(ctx_ref.at[y], ctx.at[:, lane], own_sem)
    own.start()
    sent = []
    incoming = []
    for part in (0, 1):
        which = 1 - chip if part == 0 else chip
        lines = pl.ds(pl.multiple_of(which * 2 * rows, 2 * rows), 2 * rows)
        group = []
        for dy in (1, 3, 2):
            to = (y + dy) % NY
            copy = remote(
                ctx_ref.at[to, lines], ctx.at[lines, lane],
                ctx_send.at[part, dy], ctx_recv.at[part, dy], span_at(x, to, z), sub,
            )
            copy.start()
            group.append(copy)
        sent += group
        incoming.append(group)
    own.wait()
    load.wait()
    for copy in incoming[0]:
        copy.wait_recv()

    def product(which, piece):
        lines = pl.ds(pl.multiple_of(which * 2 * rows, 2 * rows), 2 * rows)
        return jnp.dot(
            ctx[lines, :], wo[:, piece * cols : (piece + 1) * cols],
            preferred_element_type=jnp.float32,
        ).reshape(2, rows, cols)

    to_mate = []
    to_over = []
    to_relay = []

    def forward(piece):
        to_mate[piece].wait_recv()
        total = away[piece, core] + take_mate[piece].astype(jnp.float32)
        give_over[piece] = total.astype(jnp.bfloat16)
        copy = remote(
            give_over.at[piece], relay.at[piece],
            relay_send.at[piece], relay_recv.at[piece], side, over if piece % 2 else sub,
        )
        copy.start()
        to_relay.append(copy)

    def carry_on(piece):
        to_relay[piece].wait_recv()
        copy = remote(
            relay.at[piece], take_over.at[piece],
            over_send.at[piece], over_recv.at[piece], side, sub if piece % 2 else over,
        )
        copy.start()
        to_over.append(copy)

    for piece in range(pieces):
        away[piece] = product(1 - chip, piece)
        give_mate[piece] = away[piece, 1 - core].astype(jnp.bfloat16)
        copy = remote(
            give_mate.at[piece], take_mate.at[piece],
            mate_send.at[piece], mate_recv.at[piece], seq, mate,
        )
        copy.start()
        to_mate.append(copy)
        if piece:
            forward(piece - 1)
    forward(pieces - 1)

    for copy in incoming[1]:
        copy.wait_recv()
    to_home = []
    for piece in range(pieces):
        home[piece] = product(chip, piece)
        give_home[piece] = home[piece, 1 - core].astype(jnp.bfloat16)
        copy = remote(
            give_home.at[piece], take_home.at[piece],
            home_send.at[piece], home_recv.at[piece], seq, mate,
        )
        copy.start()
        to_home.append(copy)
        carry_on(piece)
    for piece in range(pieces):
        to_home[piece].wait_recv()
        to_over[piece].wait_recv()
        total = home[piece, core] + take_home[piece].astype(jnp.float32)
        total = total + take_over[piece].astype(jnp.float32)
        out_ref[:, piece * cols : (piece + 1) * cols] = total.astype(jnp.bfloat16)
    for copy in sent + to_mate + to_relay + to_over + to_home:
        copy.wait_send()


def merge(ctx, w_out):
    span = ctx.shape[1]
    rows = span // 4
    depth, width = w_out.shape
    pieces = 8
    cols = width // pieces
    dma = pltpu.SemaphoreType.DMA
    half = pltpu.VMEM((pieces, rows, cols), jnp.bfloat16)
    return pl.pallas_call(
        merge_kernel,
        out_shape=jax.ShapeDtypeStruct((rows, width), jnp.bfloat16),
        in_specs=[
            pl.BlockSpec(memory_space=pltpu.VMEM),
            pl.BlockSpec(memory_space=pl.ANY),
        ],
        out_specs=pl.BlockSpec(memory_space=pltpu.VMEM),
        scratch_shapes=[
            pltpu.VMEM((span, depth), jnp.bfloat16),
            pltpu.VMEM((depth, width), jnp.bfloat16),
            pltpu.VMEM((pieces, 2, rows, cols), jnp.float32),
            pltpu.VMEM((pieces, 2, rows, cols), jnp.float32),
            half, half, half, half, half, half, half,
            dma, dma, dma((2, NY)), dma((2, NY)),
            dma((pieces,)), dma((pieces,)), dma((pieces,)), dma((pieces,)),
            dma((pieces,)), dma((pieces,)), dma((pieces,)), dma((pieces,)),
        ],
        compiler_params=pltpu.CompilerParams(
            collective_id=1, has_side_effects=True, vmem_limit_bytes=48 * 1024 * 1024
        ),
        name="merge",
    )(ctx, w_out)


def shards(normed, w_query, w_key, w_value, w_out, pattern, slide_lengths):
    far, group = exchange(normed, w_query, w_key, w_value, pattern)
    ctx = attend(far, group, slide_lengths)
    return merge(ctx, w_out)


def solution(mesh):
    placed = (
        P(("seq", "sub"), None),
        P(None, "sub"),
        P(None, "sub"),
        P(None, "sub"),
        P("sub", None),
        P("sub", None),
        P(),
    )
    return jax.shard_map(
        shards, mesh=mesh, in_specs=placed, out_specs=P(("seq", "sub"), None), check_vma=False
    )
```

```python
import functools
import math

import jax
import jax.numpy as jnp
from jax import lax
from jax.experimental import pallas as pl
from jax.experimental.pallas import tpu as pltpu
from jax.sharding import PartitionSpec as P

HEAD = 128
BLOCK = 128
KEPT = 16
MESH = pl.DeviceIdType.MESH
NX, NY, NZ = 2, 4, 8
SPANS = NX * NY * NZ
ROW_CUTS = 4
FIRST_CUTS = 2
LOG2E = 1.4426950408889634
NSLIDE = 8
HIDE = -1e30
ORDER = (0, 1, 3, 2)


def position():
    seq = lax.axis_index("seq")
    sub = lax.axis_index("sub")
    x = seq // (NY * NZ)
    y = (seq // NZ) % NY
    z = seq % NZ
    return seq, sub, x, y, z


def span_at(x, y, z):
    return x * (NY * NZ) + y * NZ + z


def remote(src, dst, send, recv, seq, sub):
    return pltpu.make_async_remote_copy(
        src_ref=src,
        dst_ref=dst,
        send_sem=send,
        recv_sem=recv,
        device_id=(seq, sub),
        device_id_type=MESH,
    )


def greet(places):
    barrier = pltpu.get_barrier_semaphore()
    for seq, sub in places:
        pl.semaphore_signal(barrier, inc=1, device_id=(seq, sub), device_id_type=MESH)
    pl.semaphore_wait(barrier, len(places))


class Ring:
    def __init__(self, turn, early, far, sems, place, counts):
        self.turn = turn
        self.early = early
        self.late = tuple(pair for pair in (0, 1) if pair not in early)
        self.far = far
        self.mate_recv, self.recv, self.send = sems
        self.place = place
        self.counts = counts
        self.sent = []
        self.flows = [(0, 0), (0, 1)] + [(1, pair) for pair in early]
        self.upward = set(self.flows[turn::2])

    def slot(self, r, other, pair):
        index = ((self.turn * NZ + r) * 2 + other) * 2 + pair
        return self.far.at[self.turn, r, other, 2 * pair : 2 * pair + 2], self.recv.at[index]

    def launch(self, src, dst, sem, place):
        index = self.counts[0]
        self.counts[0] = index + 1
        copy = remote(src, dst, self.send.at[index], sem, place, self.place[3])
        copy.start()
        self.sent.append(copy)

    def wait(self, r, other, pair):
        x, y, z, sub = self.place
        ref, sem = self.slot(r, other, pair)
        remote(ref, ref, self.send.at[0], sem, span_at(1 - x, y, z), sub).wait_recv()

    def put_x(self, r, pair):
        x, y, z, sub = self.place
        dst, sem = self.slot(r, 1, pair)
        self.launch(self.slot(r, 0, pair)[0], dst, sem, span_at(1 - x, y, z))

    def put_z(self, r, other, pair, step):
        x, y, z, sub = self.place
        dst, sem = self.slot((r - step) % NZ, other, pair)
        self.launch(self.slot(r, other, pair)[0], dst, sem, span_at(x, y, (z + step + NZ) % NZ))

    def begin(self, dil, own_sem):
        x, y, z, sub = self.place
        self.own = pltpu.make_async_copy(dil.at[y], self.far.at[self.turn, 0, 0, 0], own_sem)
        self.own.start()
        self.mates = []
        for dy in ORDER[1:]:
            head = (y + dy) % NY
            at = ORDER.index((NY - dy) % NY)
            dst = self.far.at[self.turn, 0, 0, at]
            self.launch(dil.at[head], dst, self.mate_recv.at[self.turn * NY + at], span_at(x, head, z))

    def wait_mate(self, at):
        x, y, z, sub = self.place
        dst = self.far.at[self.turn, 0, 0, at]
        remote(
            dst, dst, self.send.at[0], self.mate_recv.at[self.turn * NY + at],
            span_at(x, (y + 1) % NY, z), sub,
        ).wait_recv()

    def serve(self, d, others=(0, 1)):
        if d == 0:
            if 0 in others:
                self.own.wait()
                for pair in (0, 1):
                    for at in (2 * pair, 2 * pair + 1):
                        if at:
                            self.wait_mate(at)
                    self.put_x(0, pair)
                    self.put_z(0, 0, pair, 1)
                    self.put_z(0, 0, pair, -1)
            if 1 in others:
                for pair in self.early:
                    self.wait(0, 1, pair)
                    self.put_z(0, 1, pair, 1)
                    self.put_z(0, 1, pair, -1)
            return
        for flow in self.flows:
            other, pair = flow
            if other not in others:
                continue
            for up in (True, False):
                if d == 4 and up != (flow in self.upward):
                    continue
                r = NZ - d if up else d
                self.wait(r, other, pair)
                if d < 3 or (d == 3 and up == (flow in self.upward)):
                    self.put_z(r, other, pair, 1 if up else -1)
                if other == 0 and pair in self.late:
                    self.put_x(r, pair)

    def serve_late(self, d):
        for pair in self.late:
            for r in {0: (0,), 4: (4,)}.get(d, (NZ - d, d)):
                self.wait(r, 1, pair)


def exchange_kernel(
    len_ref, x_hbm, wq_hbm, wk_hbm, wv_hbm, wo_hbm, pat_ref, out_ref,
    xs, ws, qkv, pick, dil, far, group, keyed, turned, query, acc, peak,
    ctx_own, ctx, wo, away, home, give_mate, give_over, give_home, take_mate, take_over, take_home,
    local_sem, w_sem, own_sem, own_group_sem,
    mate_send, mate_recv, cross_send, cross_recv, pass_send, pass_recv,
    group_send, group_recv, near_recv, far_recv, ring_send,
    wo_sem, own_ctx_sem, ctx_send, ctx_recv,
    sum_send, sum_recv, over_send, over_recv, home_send, home_recv,
):
    seq, sub, x, y, z = position()
    core = sub % 2
    chip = sub // 2
    mate = sub + 1 - 2 * core
    over = (sub + 2) % 4
    rows = xs.shape[1]
    cut = rows // ROW_CUTS
    side_rows = 2 * rows
    span = 4 * rows
    blocks = span // BLOCK
    factor = LOG2E / math.sqrt(HEAD)

    own_x = pltpu.make_async_copy(x_hbm, xs.at[sub], local_sem)
    own_x.start()
    weights = []
    for index, (source, half) in enumerate(
        [(wk_hbm, 0), (wk_hbm, 1), (wv_hbm, 0), (wv_hbm, 1), (wq_hbm, 0), (wq_hbm, 1)]
    ):
        copy = pltpu.make_async_copy(
            source.at[:, half * 256 : (half + 1) * 256], ws.at[index], w_sem.at[index]
        )
        copy.start()
        weights.append(copy)

    load = pltpu.make_async_copy(wo_hbm, wo, wo_sem)
    load.start()
    side = span_at(1 - x, y, z)
    above = span_at(x, y, (z + 1) % NZ)
    below = span_at(x, y, (z + NZ - 1) % NZ)
    fellows = [span_at(x, (y + dy) % NY, z) for dy in (1, 2, 3)]
    greet(
        [(seq, mate), (seq, over), (side, sub), (above, sub), (below, sub)]
        + [(fellow, sub) for fellow in fellows]
    )

    to_mate = remote(x_hbm, xs.at[sub], mate_send, mate_recv, seq, mate)
    to_mate.start()
    crossing = []

    def cross(cuts):
        for r in cuts:
            part = slice(r * cut, (r + 1) * cut)
            copy = remote(
                x_hbm.at[part], xs.at[sub, part], cross_send.at[r], cross_recv.at[r], seq, over
            )
            copy.start()
            crossing.append(copy)

    cross(range(FIRST_CUTS))

    line = lax.broadcasted_iota(jnp.int32, (BLOCK, BLOCK), 0)
    for head in range(NY):
        hit = (line == pat_ref[head : head + 1, :]).astype(jnp.float32)
        pick[head] = hit.T[:KEPT, :].astype(jnp.bfloat16)

    def project(which, indices):
        lhs = xs[pl.ds(2 * which, 2)].reshape(side_rows, xs.shape[2])
        for index in indices:
            out = jnp.dot(lhs, ws[index], preferred_element_type=jnp.float32)
            if index > 3:
                out = out * factor
            out = out.astype(jnp.bfloat16)
            kind = (1, 2, 0)[index // 2]
            first = 2 * (index % 2)
            qkv[first, which, kind] = out[:, :HEAD]
            qkv[first + 1, which, kind] = out[:, HEAD:]

    half = 2 * KEPT

    def choose(which, into):
        for head in range(NY):
            for kind in (1, 2):
                for b in range(2):
                    taken = jnp.dot(
                        pick[head],
                        qkv[head, which, kind, b * BLOCK : (b + 1) * BLOCK, :],
                        preferred_element_type=jnp.float32,
                    )
                    base = (kind - 1) * half + b * KEPT
                    dil[into, head, base : base + KEPT, :] = taken.astype(jnp.bfloat16)

    counts = [0]
    sems = (near_recv, far_recv, ring_send)
    place = (x, y, z, sub)
    rings = [
        Ring(0, (0, 1), far, sems, place, counts),
        Ring(1, (0,), far, sems, place, counts),
    ]
    group_sent = []

    def share(which, turn):
        own = pltpu.make_async_copy(
            qkv.at[y, which], group.at[y, which], own_group_sem.at[turn]
        )
        own.start()
        for k, kinds in enumerate((slice(0, 1), slice(1, 3))):
            for dy in (1, 3, 2):
                head = (y + dy) % NY
                copy = remote(
                    qkv.at[head, which, kinds], group.at[y, which, kinds],
                    group_send.at[4 * dy + 2 * turn + k], group_recv.at[4 * y + 2 * which + k],
                    span_at(x, head, z), sub,
                )
                copy.start()
                group_sent.append(copy)
        return own

    def got_group(dy, k):
        fellow = (y + dy) % NY
        kinds = slice(1, 3) if k else slice(0, 1)
        for which in (chip, 1 - chip):
            remote(
                qkv.at[fellow, which, kinds], group.at[fellow, which, kinds],
                group_send.at[4], group_recv.at[4 * fellow + 2 * which + k],
                span_at(x, fellow, z), sub,
            ).wait_recv()

    own_x.wait()
    to_mate.wait_recv()
    for index in range(4):
        weights[index].wait()
    project(chip, range(4))
    choose(chip, 0)
    rings[0].begin(dil.at[0], own_sem.at[0])
    weights[4].wait()
    weights[5].wait()
    project(chip, (4, 5))
    own_groups = [share(chip, 0)]
    rings[0].serve(0, (0,))
    cross(range(FIRST_CUTS, ROW_CUTS))

    col = lax.broadcasted_iota(jnp.int32, (1, HEAD), 1)
    low = (col - NSLIDE) * blocks
    high = low + blocks
    total = jnp.int32(0)
    for j in range(NSLIDE):
        low = jnp.where(col == j, total, low)
        total = total + len_ref[j]
        high = jnp.where(col == j, total, high)
    flag = jnp.where(col < NSLIDE, 1.0, 0.0)
    line = lax.broadcasted_iota(jnp.int32, (span, HEAD), 0)

    def inside(block):
        return jnp.where((block >= low) & (block < high), 1.0, 0.0)

    pairs = [(turn, a, b) for turn in (0, 1) for a, b in ((7, 1), (6, 2), (5, 3), (0, 4))]
    turned[:, HEAD:, :] = jnp.ones((turned.shape[0], 16, span), jnp.bfloat16)

    def mark_chunk(c):
        turn, ra, rb = pairs[c]
        which = 1 - chip if turn else chip
        at = line % 128 // half
        at = jnp.where(at == 2, 3, jnp.where(at == 3, 2, at))
        away = jnp.where(line < 256, ra, rb)
        owner = span_at((x + line % 256 // 128) % NX, (y + at) % NY, (z + away) % NZ)
        block = owner * blocks + 2 * which + line % half // KEPT
        keyed[c, :, HEAD:] = (HIDE * jnp.abs(inside(block) - flag)).astype(jnp.bfloat16)

    def mark_span(item):
        mine = span_at(x, item, z)
        got = inside(mine * blocks + line // BLOCK)
        mark = flag * got + jnp.where(col == NSLIDE + mine, 1.0, 0.0)
        query[item, HEAD:, :] = mark.astype(jnp.bfloat16).T
        keyed[8 + item, :, HEAD:] = (HIDE * (flag * (1.0 - got))).astype(jnp.bfloat16)

    passing = []

    def hand_on(r):
        part = slice(r * cut, (r + 1) * cut)
        crossing[r].wait_recv()
        copy = remote(
            xs.at[over, part], xs.at[over, part], pass_send.at[r], pass_recv.at[r], seq, mate
        )
        copy.start()
        passing.append(copy)

    def marks(step):
        for c in (2 * step, 2 * step + 1):
            mark_chunk(c)
        mark_span(step)

    first, second = rings
    marks(0)
    first.serve(1, (0,))
    hand_on(0)
    marks(1)
    first.serve(2, (0,))
    hand_on(1)
    marks(2)
    first.serve(0, (1,))
    first.serve(3, (0,))
    hand_on(2)
    marks(3)
    acc[...] = jnp.zeros_like(acc)
    peak[...] = jnp.full_like(peak, 3 * HIDE)
    first.serve(1, (1,))
    first.serve(4, (0,))
    hand_on(3)
    for copy in passing:
        copy.wait_recv()
    project(1 - chip, range(4))
    choose(1 - chip, 1)
    second.begin(dil.at[1], own_sem.at[1])
    project(1 - chip, (4, 5))
    own_groups.append(share(1 - chip, 1))
    first.serve(2, (1,))

    def load_chunk(c):
        turn, ra, rb = pairs[c]
        for k, r in enumerate((ra, rb)):
            lines = slice(256 * k, 256 * (k + 1))
            keyed[c, lines, :HEAD] = far[turn, r, :, :, :half, :].reshape(256, HEAD)
            turned[c, :HEAD, lines] = far[turn, r, :, :, half:, :].reshape(256, HEAD).T

    def load_query(item):
        query[item, :HEAD, :] = group[item, :, 0].reshape(span, HEAD).T

    def load_near(item):
        keyed[8 + item, :, :HEAD] = group[item, :, 1].reshape(span, HEAD)
        turned[8 + item, :HEAD, :] = group[item, :, 2].reshape(span, HEAD).T

    def update(item, chunks):
        ask = query[item]
        found = [jnp.dot(keyed[c], ask, preferred_element_type=jnp.float32) for c in chunks]
        old = peak[item, :1, :]
        top = old
        for got in found:
            top = jnp.maximum(top, jnp.max(got, axis=0, keepdims=True))
        out = acc[item] * jnp.exp2(old - top)
        for c, got in zip(chunks, found):
            weight = jnp.exp2(got - top).astype(jnp.bfloat16)
            out = out + jnp.dot(turned[c], weight, preferred_element_type=jnp.float32)
        acc[item] = out
        peak[item] = jnp.broadcast_to(top, peak.shape[1:])

    def repeat(count, body):
        def step(k, carry):
            body(k)
            return carry

        lax.fori_loop(0, count, step, 0)

    for own in own_groups:
        own.wait()
    load_query(y)
    load_near(y)
    first.serve(3, (1,))
    second.serve(0, (0,))
    first.serve(4, (1,))
    second.serve(0, (1,))
    for c in range(4):
        load_chunk(c)
    repeat(2, lambda k: update(y, (2 * k, 2 * k + 1)))
    second.serve(1)
    second.serve_late(0)
    for dy in (1, 3):
        got_group(dy, 0)
        load_query((y + dy) % NY)
    repeat(2, lambda k: update((y + 1) % NY, (2 * k, 2 * k + 1)))
    second.serve(2)
    second.serve_late(1)
    repeat(2, lambda k: update((y + 3) % NY, (2 * k, 2 * k + 1)))
    got_group(2, 0)
    load_query((y + 2) % NY)
    second.serve(3)
    second.serve_late(2)
    load_chunk(4)
    load_chunk(5)
    repeat(2, lambda k: update((y + 2) % NY, (2 * k, 2 * k + 1)))
    second.serve(4)
    repeat(4, lambda k: update(k, (4, 5)))
    for dy in (1, 3, 2):
        got_group(dy, 1)
        load_near((y + dy) % NY)
    second.serve_late(3)
    load_chunk(6)
    repeat(4, lambda k: update(k, (6, 8 + k)))
    second.serve_late(4)
    load_chunk(7)

    def finish(item):
        update(item, (7,))
        out = acc[item, :HEAD, :] / acc[item, HEAD : HEAD + 1, :]
        ctx_own[item] = out.T.astype(jnp.bfloat16)

    pieces = away.shape[0]
    cols = away.shape[3]
    lane = pl.ds(pl.multiple_of(y * HEAD, HEAD), HEAD)
    sent = []
    incoming = [[], []]
    for dy in (1, 3, 2, 0):
        to = (y + dy) % NY
        finish(to)
        if dy == 0:
            own = pltpu.make_async_copy(ctx_own.at[y], ctx.at[:, lane], own_ctx_sem)
            own.start()
            continue
        for part in (0, 1):
            which = 1 - chip if part == 0 else chip
            lines = pl.ds(pl.multiple_of(which * 2 * rows, 2 * rows), 2 * rows)
            copy = remote(
                ctx_own.at[to, lines], ctx.at[lines, lane],
                ctx_send.at[2 * dy + part], ctx_recv.at[2 * dy + part], span_at(x, to, z), sub,
            )
            copy.start()
            sent.append(copy)
            incoming[part].append(copy)
    own.wait()
    load.wait()
    for copy in incoming[0]:
        copy.wait_recv()

    def product(which, piece):
        lines = pl.ds(pl.multiple_of(which * 2 * rows, 2 * rows), 2 * rows)
        return jnp.dot(
            ctx[lines, :], wo[:, piece * cols : (piece + 1) * cols],
            preferred_element_type=jnp.float32,
        ).reshape(2, rows, cols)

    to_partner = []
    to_over = []

    def forward(piece):
        to_partner[piece].wait_recv()
        total = away[piece, core] + take_mate[piece].astype(jnp.float32)
        give_over[piece] = total.astype(jnp.bfloat16)
        copy = remote(
            give_over.at[piece], take_over.at[piece],
            over_send.at[piece], over_recv.at[piece], seq, over,
        )
        copy.start()
        to_over.append(copy)

    for piece in range(pieces):
        away[piece] = product(1 - chip, piece)
        give_mate[piece] = away[piece, 1 - core].astype(jnp.bfloat16)
        copy = remote(
            give_mate.at[piece], take_mate.at[piece],
            sum_send.at[piece], sum_recv.at[piece], seq, mate,
        )
        copy.start()
        to_partner.append(copy)
        if piece:
            forward(piece - 1)
    forward(pieces - 1)

    for copy in incoming[1]:
        copy.wait_recv()
    to_home = []
    for piece in range(pieces):
        home[piece] = product(chip, piece)
        give_home[piece] = home[piece, 1 - core].astype(jnp.bfloat16)
        copy = remote(
            give_home.at[piece], take_home.at[piece],
            home_send.at[piece], home_recv.at[piece], seq, mate,
        )
        copy.start()
        to_home.append(copy)
    for piece in range(pieces):
        to_home[piece].wait_recv()
        to_over[piece].wait_recv()
        total = home[piece, core] + take_home[piece].astype(jnp.float32)
        total = total + take_over[piece].astype(jnp.float32)
        out_ref[:, piece * cols : (piece + 1) * cols] = total.astype(jnp.bfloat16)
    waiting = sent + to_partner + to_over + to_home
    for copy in waiting + [to_mate] + crossing + passing + group_sent + rings[0].sent + rings[1].sent:
        copy.wait_send()


def exchange(normed, w_query, w_key, w_value, w_out, pattern, slide_lengths):
    rows, width = normed.shape
    depth = w_out.shape[0]
    pieces = 4
    cols = width // pieces
    span = 4 * rows
    kept = 4 * KEPT
    any_spec = pl.BlockSpec(memory_space=pltpu.HBM)
    vmem_spec = pl.BlockSpec(memory_space=pltpu.VMEM)
    dma = pltpu.SemaphoreType.DMA
    vmem = pltpu.VMEM
    sums = vmem((pieces, 2, rows, cols), jnp.float32)
    parts = vmem((pieces, rows, cols), jnp.bfloat16)
    return pl.pallas_call(
        exchange_kernel,
        out_shape=jax.ShapeDtypeStruct((rows, width), jnp.bfloat16),
        in_specs=[pl.BlockSpec(memory_space=pltpu.SMEM)] + [any_spec] * 5 + [vmem_spec],
        out_specs=vmem_spec,
        scratch_shapes=[
            vmem((4, rows, width), jnp.bfloat16),
            vmem((6, width, 256), jnp.bfloat16),
            vmem((NY, 2, 3, span // 2, HEAD), jnp.bfloat16),
            vmem((NY, KEPT, BLOCK), jnp.bfloat16),
            vmem((2, NY, kept, HEAD), jnp.bfloat16),
            vmem((2, NZ, NX, NY, kept, HEAD), jnp.bfloat16),
            vmem((NY, 2, 3, span // 2, HEAD), jnp.bfloat16),
            vmem((8 + NY, span, 2 * HEAD), jnp.bfloat16),
            vmem((8 + NY, HEAD + 16, span), jnp.bfloat16),
            vmem((NY, 2 * HEAD, span), jnp.bfloat16),
            vmem((NY, HEAD + 16, span), jnp.float32),
            vmem((NY, 8, span), jnp.float32),
            vmem((NY, span, HEAD), jnp.bfloat16),
            vmem((span, depth), jnp.bfloat16),
            vmem((depth, width), jnp.bfloat16),
            sums, sums, parts, parts, parts, parts, parts, parts,
            dma, dma((6,)), dma((2,)), dma((2,)),
            dma, dma, dma((ROW_CUTS,)), dma((ROW_CUTS,)), dma((ROW_CUTS,)), dma((ROW_CUTS,)),
            dma((4 * NY,)), dma((4 * NY,)), dma((2 * NY,)), dma((4 * 2 * NZ,)), dma((80,)),
            dma, dma, dma((2 * NY,)), dma((2 * NY,)),
            dma((pieces,)), dma((pieces,)), dma((pieces,)), dma((pieces,)),
            dma((pieces,)), dma((pieces,)),
        ],
        compiler_params=pltpu.CompilerParams(
            collective_id=0, has_side_effects=True, vmem_limit_bytes=67043328
        ),
        name="exchange",
    )(slide_lengths, normed, w_query, w_key, w_value, w_out, pattern)


def shards(normed, w_query, w_key, w_value, w_out, pattern, slide_lengths):
    return exchange(normed, w_query, w_key, w_value, w_out, pattern, slide_lengths)


def solution(mesh):
    placed = (
        P(("seq", "sub"), None),
        P(None, "sub"),
        P(None, "sub"),
        P(None, "sub"),
        P("sub", None),
        P("sub", None),
        P(),
    )
    return jax.shard_map(
        shards, mesh=mesh, in_specs=placed, out_specs=P(("seq", "sub"), None), check_vma=False
    )
```

```python
import functools
import math

import jax
import jax.numpy as jnp
from jax import lax
from jax.experimental import pallas as pl
from jax.experimental.pallas import tpu as pltpu
from jax.sharding import PartitionSpec as P

HEAD = 128
BLOCK = 128
KEPT = 16
MESH = pl.DeviceIdType.MESH
NX, NY, NZ = 2, 4, 8
SPANS = NX * NY * NZ
ROW_CUTS = 4
FIRST_CUTS = 2
LOG2E = 1.4426950408889634
NSLIDE = 8
HIDE = -1e30
ORDER = (0, 1, 3, 2)


def position():
    seq = lax.axis_index("seq")
    sub = lax.axis_index("sub")
    x = seq // (NY * NZ)
    y = (seq // NZ) % NY
    z = seq % NZ
    return seq, sub, x, y, z


def span_at(x, y, z):
    return x * (NY * NZ) + y * NZ + z


def remote(src, dst, send, recv, seq, sub):
    return pltpu.make_async_remote_copy(
        src_ref=src,
        dst_ref=dst,
        send_sem=send,
        recv_sem=recv,
        device_id=(seq, sub),
        device_id_type=MESH,
    )


def greet(places):
    barrier = pltpu.get_barrier_semaphore()
    for seq, sub in places:
        pl.semaphore_signal(barrier, inc=1, device_id=(seq, sub), device_id_type=MESH)
    pl.semaphore_wait(barrier, len(places))


class Ring:
    def __init__(self, turn, early, far, sems, place, counts):
        self.turn = turn
        self.early = early
        self.late = tuple(pair for pair in (0, 1) if pair not in early)
        self.far = far
        self.mate_recv, self.recv, self.send = sems
        self.place = place
        self.counts = counts
        self.sent = []
        self.flows = [(0, 0), (0, 1)] + [(1, pair) for pair in early]
        self.upward = set(self.flows[turn::2])

    def slot(self, r, other, pair):
        index = ((self.turn * NZ + r) * 2 + other) * 2 + pair
        return self.far.at[self.turn, r, other, 2 * pair : 2 * pair + 2], self.recv.at[index]

    def launch(self, src, dst, sem, place):
        index = self.counts[0]
        self.counts[0] = index + 1
        copy = remote(src, dst, self.send.at[index], sem, place, self.place[3])
        copy.start()
        self.sent.append(copy)

    def wait(self, r, other, pair):
        x, y, z, sub = self.place
        ref, sem = self.slot(r, other, pair)
        remote(ref, ref, self.send.at[0], sem, span_at(1 - x, y, z), sub).wait_recv()

    def put_x(self, r, pair):
        x, y, z, sub = self.place
        dst, sem = self.slot(r, 1, pair)
        self.launch(self.slot(r, 0, pair)[0], dst, sem, span_at(1 - x, y, z))

    def put_z(self, r, other, pair, step):
        x, y, z, sub = self.place
        dst, sem = self.slot((r - step) % NZ, other, pair)
        self.launch(self.slot(r, other, pair)[0], dst, sem, span_at(x, y, (z + step + NZ) % NZ))

    def begin(self, dil, own_sem):
        x, y, z, sub = self.place
        self.own = pltpu.make_async_copy(dil.at[y], self.far.at[self.turn, 0, 0, 0], own_sem)
        self.own.start()
        self.mates = []
        for dy in ORDER[1:]:
            head = (y + dy) % NY
            at = ORDER.index((NY - dy) % NY)
            dst = self.far.at[self.turn, 0, 0, at]
            self.launch(dil.at[head], dst, self.mate_recv.at[self.turn * NY + at], span_at(x, head, z))

    def wait_mate(self, at):
        x, y, z, sub = self.place
        dst = self.far.at[self.turn, 0, 0, at]
        remote(
            dst, dst, self.send.at[0], self.mate_recv.at[self.turn * NY + at],
            span_at(x, (y + 1) % NY, z), sub,
        ).wait_recv()

    def serve(self, d, others=(0, 1)):
        if d == 0:
            if 0 in others:
                self.own.wait()
                for pair in (0, 1):
                    for at in (2 * pair, 2 * pair + 1):
                        if at:
                            self.wait_mate(at)
                    self.put_x(0, pair)
                    self.put_z(0, 0, pair, 1)
                    self.put_z(0, 0, pair, -1)
            if 1 in others:
                for pair in self.early:
                    self.wait(0, 1, pair)
                    self.put_z(0, 1, pair, 1)
                    self.put_z(0, 1, pair, -1)
            return
        for flow in self.flows:
            other, pair = flow
            if other not in others:
                continue
            for up in (True, False):
                if d == 4 and up != (flow in self.upward):
                    continue
                r = NZ - d if up else d
                self.wait(r, other, pair)
                if d < 3 or (d == 3 and up == (flow in self.upward)):
                    self.put_z(r, other, pair, 1 if up else -1)
                if other == 0 and pair in self.late:
                    self.put_x(r, pair)

    def serve_late(self, d):
        for pair in self.late:
            for r in {0: (0,), 4: (4,)}.get(d, (NZ - d, d)):
                self.wait(r, 1, pair)


def exchange_kernel(
    len_ref, x_hbm, wq_hbm, wk_hbm, wv_hbm, wo_hbm, pat_ref, out_ref,
    xs, ws, qkv, pick, dil, far, group, keyed, turned, query, acc, peak,
    ctx_own, ctx, wo, away, home, give_mate, give_over, give_home, take_mate, take_over, take_home,
    local_sem, w_sem, own_sem, own_group_sem,
    mate_send, mate_recv, cross_send, cross_recv, pass_send, pass_recv,
    group_send, group_recv, near_recv, far_recv, ring_send,
    wo_sem, own_ctx_sem, ctx_send, ctx_recv,
    sum_send, sum_recv, over_send, over_recv, home_send, home_recv,
):
    seq, sub, x, y, z = position()
    core = sub % 2
    chip = sub // 2
    mate = sub + 1 - 2 * core
    over = (sub + 2) % 4
    rows = xs.shape[1]
    cut = rows // ROW_CUTS
    side_rows = 2 * rows
    span = 4 * rows
    blocks = span // BLOCK
    factor = LOG2E / math.sqrt(HEAD)

    own_x = pltpu.make_async_copy(x_hbm, xs.at[sub], local_sem)
    own_x.start()
    weights = []
    for index, (source, half) in enumerate(
        [(wk_hbm, 0), (wk_hbm, 1), (wv_hbm, 0), (wv_hbm, 1), (wq_hbm, 0), (wq_hbm, 1)]
    ):
        copy = pltpu.make_async_copy(
            source.at[:, half * 256 : (half + 1) * 256], ws.at[index], w_sem.at[index]
        )
        copy.start()
        weights.append(copy)

    load = pltpu.make_async_copy(wo_hbm, wo, wo_sem)
    load.start()
    side = span_at(1 - x, y, z)
    above = span_at(x, y, (z + 1) % NZ)
    below = span_at(x, y, (z + NZ - 1) % NZ)
    fellows = [span_at(x, (y + dy) % NY, z) for dy in (1, 2, 3)]
    greet(
        [(seq, mate), (seq, over), (side, sub), (above, sub), (below, sub)]
        + [(fellow, sub) for fellow in fellows]
    )

    to_mate = remote(x_hbm, xs.at[sub], mate_send, mate_recv, seq, mate)
    to_mate.start()
    crossing = []

    def cross(cuts):
        for r in cuts:
            part = slice(r * cut, (r + 1) * cut)
            copy = remote(
                x_hbm.at[part], xs.at[sub, part], cross_send.at[r], cross_recv.at[r], seq, over
            )
            copy.start()
            crossing.append(copy)

    cross(range(FIRST_CUTS))

    line = lax.broadcasted_iota(jnp.int32, (BLOCK, BLOCK), 0)
    for head in range(NY):
        hit = (line == pat_ref[head : head + 1, :]).astype(jnp.float32)
        pick[head] = hit.T[:KEPT, :].astype(jnp.bfloat16)

    def project(which, indices):
        lhs = xs[pl.ds(2 * which, 2)].reshape(side_rows, xs.shape[2])
        for index in indices:
            out = jnp.dot(lhs, ws[index], preferred_element_type=jnp.float32)
            if index > 3:
                out = out * factor
            out = out.astype(jnp.bfloat16)
            kind = (1, 2, 0)[index // 2]
            first = 2 * (index % 2)
            qkv[first, which, kind] = out[:, :HEAD]
            qkv[first + 1, which, kind] = out[:, HEAD:]

    half = 2 * KEPT

    def choose(which, into):
        for head in range(NY):
            for kind in (1, 2):
                for b in range(2):
                    taken = jnp.dot(
                        pick[head],
                        qkv[head, which, kind, b * BLOCK : (b + 1) * BLOCK, :],
                        preferred_element_type=jnp.float32,
                    )
                    base = (kind - 1) * half + b * KEPT
                    dil[into, head, base : base + KEPT, :] = taken.astype(jnp.bfloat16)

    counts = [0]
    sems = (near_recv, far_recv, ring_send)
    place = (x, y, z, sub)
    rings = [
        Ring(0, (0, 1), far, sems, place, counts),
        Ring(1, (0,), far, sems, place, counts),
    ]
    group_sent = []

    def share(which, turn):
        own = pltpu.make_async_copy(
            qkv.at[y, which], group.at[y, which], own_group_sem.at[turn]
        )
        own.start()
        for k, kinds in enumerate((slice(0, 1), slice(1, 3))):
            for dy in (1, 3, 2):
                head = (y + dy) % NY
                copy = remote(
                    qkv.at[head, which, kinds], group.at[y, which, kinds],
                    group_send.at[4 * dy + 2 * turn + k], group_recv.at[4 * y + 2 * which + k],
                    span_at(x, head, z), sub,
                )
                copy.start()
                group_sent.append(copy)
        return own

    def got_group(dy, k):
        fellow = (y + dy) % NY
        kinds = slice(1, 3) if k else slice(0, 1)
        for which in (chip, 1 - chip):
            remote(
                qkv.at[fellow, which, kinds], group.at[fellow, which, kinds],
                group_send.at[4], group_recv.at[4 * fellow + 2 * which + k],
                span_at(x, fellow, z), sub,
            ).wait_recv()

    own_x.wait()
    to_mate.wait_recv()
    for index in range(4):
        weights[index].wait()
    project(chip, range(4))
    choose(chip, 0)
    rings[0].begin(dil.at[0], own_sem.at[0])
    weights[4].wait()
    weights[5].wait()
    project(chip, (4, 5))
    own_groups = [share(chip, 0)]
    rings[0].serve(0, (0,))
    cross(range(FIRST_CUTS, ROW_CUTS))

    col = lax.broadcasted_iota(jnp.int32, (1, HEAD), 1)
    low = (col - NSLIDE) * blocks
    high = low + blocks
    total = jnp.int32(0)
    for j in range(NSLIDE):
        low = jnp.where(col == j, total, low)
        total = total + len_ref[j]
        high = jnp.where(col == j, total, high)
    flag = jnp.where(col < NSLIDE, 1.0, 0.0)
    line = lax.broadcasted_iota(jnp.int32, (span, HEAD), 0)

    def inside(block):
        return jnp.where((block >= low) & (block < high), 1.0, 0.0)

    pairs = [(turn, a, b) for turn in (0, 1) for a, b in ((7, 1), (6, 2), (5, 3), (0, 4))]
    turned[:, HEAD:, :] = jnp.ones((turned.shape[0], 16, span), jnp.bfloat16)

    def mark_chunk(c):
        turn, ra, rb = pairs[c]
        which = 1 - chip if turn else chip
        at = line % 128 // half
        at = jnp.where(at == 2, 3, jnp.where(at == 3, 2, at))
        away = jnp.where(line < 256, ra, rb)
        owner = span_at((x + line % 256 // 128) % NX, (y + at) % NY, (z + away) % NZ)
        block = owner * blocks + 2 * which + line % half // KEPT
        keyed[c, :, HEAD:] = (HIDE * jnp.abs(inside(block) - flag)).astype(jnp.bfloat16)

    def mark_span(item):
        mine = span_at(x, item, z)
        got = inside(mine * blocks + line // BLOCK)
        mark = flag * got + jnp.where(col == NSLIDE + mine, 1.0, 0.0)
        query[item, HEAD:, :] = mark.astype(jnp.bfloat16).T
        keyed[8 + item, :, HEAD:] = (HIDE * (flag * (1.0 - got))).astype(jnp.bfloat16)

    passing = []

    def hand_on(r):
        part = slice(r * cut, (r + 1) * cut)
        crossing[r].wait_recv()
        copy = remote(
            xs.at[over, part], xs.at[over, part], pass_send.at[r], pass_recv.at[r], seq, mate
        )
        copy.start()
        passing.append(copy)

    def marks(step):
        for c in (2 * step, 2 * step + 1):
            mark_chunk(c)
        mark_span(step)

    first, second = rings
    marks(0)
    first.serve(1, (0,))
    hand_on(0)
    marks(1)
    first.serve(2, (0,))
    hand_on(1)
    marks(2)
    first.serve(0, (1,))
    first.serve(3, (0,))
    hand_on(2)
    marks(3)
    acc[...] = jnp.zeros_like(acc)
    peak[...] = jnp.full_like(peak, 3 * HIDE)
    first.serve(1, (1,))
    hand_on(3)
    for copy in passing:
        copy.wait_recv()
    project(1 - chip, range(4))
    choose(1 - chip, 1)
    second.begin(dil.at[1], own_sem.at[1])
    project(1 - chip, (4, 5))
    own_groups.append(share(1 - chip, 1))
    first.serve(2, (1,))

    def load_chunk(c):
        turn, ra, rb = pairs[c]
        for k, r in enumerate((ra, rb)):
            lines = slice(256 * k, 256 * (k + 1))
            keyed[c, lines, :HEAD] = far[turn, r, :, :, :half, :].reshape(256, HEAD)
            turned[c, :HEAD, lines] = far[turn, r, :, :, half:, :].reshape(256, HEAD).T

    def load_query(item):
        query[item, :HEAD, :] = group[item, :, 0].reshape(span, HEAD).T

    def load_near(item):
        keyed[8 + item, :, :HEAD] = group[item, :, 1].reshape(span, HEAD)
        turned[8 + item, :HEAD, :] = group[item, :, 2].reshape(span, HEAD).T

    def update(*tasks):
        state = []
        for item, chunks in tasks:
            ask = query[item]
            found = [jnp.dot(keyed[c], ask, preferred_element_type=jnp.float32) for c in chunks]
            state.append((acc[item], peak[item, :1, :], found))
        done = []
        for (item, chunks), (total, old, found) in zip(tasks, state):
            top = old
            for got in found:
                top = jnp.maximum(top, jnp.max(got, axis=0, keepdims=True))
            out = total * jnp.exp2(old - top)
            for c, got in zip(chunks, found):
                weight = jnp.exp2(got - top).astype(jnp.bfloat16)
                out = out + jnp.dot(turned[c], weight, preferred_element_type=jnp.float32)
            done.append((out, top))
        for (item, chunks), (out, top) in zip(tasks, done):
            acc[item] = out
            peak[item] = jnp.broadcast_to(top, peak.shape[1:])

    def both(first_item, second_item, chunk_of):
        return update(
            (first_item, (chunk_of(first_item),)), (second_item, (chunk_of(second_item),))
        )

    def repeat(count, body):
        def step(k, carry):
            body(k)
            return carry

        lax.fori_loop(0, count, step, 0)

    for own in own_groups:
        own.wait()
    after, before, across = (y + 1) % NY, (y + 3) % NY, (y + 2) % NY
    load_query(y)
    load_near(y)
    load_chunk(0)
    update((y, (8 + y, 0)))
    second.serve(0, (0,))
    first.serve(3, (1,))
    load_chunk(1)
    load_chunk(2)
    update((y, (1, 2)))
    second.serve(0, (1,))
    second.serve(1, (0,))
    for dy in (1, 3):
        got_group(dy, 0)
        load_query((y + dy) % NY)
    both(after, before, lambda item: 0)
    second.serve(1, (1,))
    second.serve_late(0)
    first.serve(4)
    load_chunk(3)
    repeat(2, lambda k: both(after, before, lambda item: 1 + k))
    second.serve(2)
    second.serve_late(1)
    got_group(2, 0)
    load_query(across)
    repeat(2, lambda k: update((across, (2 * k, 2 * k + 1))))
    second.serve(3)
    second.serve_late(2)
    load_chunk(4)
    load_chunk(5)
    both(after, before, lambda item: 3)
    second.serve(4)
    repeat(4, lambda k: both(k // 2 * 2, k // 2 * 2 + 1, lambda item: 4 + k % 2))
    for dy in (1, 3, 2):
        got_group(dy, 1)
        load_near((y + dy) % NY)
    both(after, across, lambda item: 8 + item)
    update((before, (8 + before,)), (y, (3,)))
    second.serve_late(3)
    load_chunk(6)
    repeat(2, lambda k: both(2 * k, 2 * k + 1, lambda item: 6))
    second.serve_late(4)
    load_chunk(7)

    def finish(item):
        out = acc[item, :HEAD, :] / acc[item, HEAD : HEAD + 1, :]
        ctx_own[item] = out.T.astype(jnp.bfloat16)

    pieces = away.shape[0]
    cols = away.shape[3]
    lane = pl.ds(pl.multiple_of(y * HEAD, HEAD), HEAD)
    sent = []
    incoming = [[], []]
    for dy in (1, 3, 2, 0):
        to = (y + dy) % NY
        if dy in (1, 2):
            both(to, (y + (3 if dy == 1 else 0)) % NY, lambda item: 7)
        finish(to)
        if dy == 0:
            own = pltpu.make_async_copy(ctx_own.at[y], ctx.at[:, lane], own_ctx_sem)
            own.start()
            continue
        for part in (0, 1):
            which = 1 - chip if part == 0 else chip
            lines = pl.ds(pl.multiple_of(which * 2 * rows, 2 * rows), 2 * rows)
            copy = remote(
                ctx_own.at[to, lines], ctx.at[lines, lane],
                ctx_send.at[2 * dy + part], ctx_recv.at[2 * dy + part], span_at(x, to, z), sub,
            )
            copy.start()
            sent.append(copy)
            incoming[part].append(copy)
    own.wait()
    load.wait()
    for copy in incoming[0]:
        copy.wait_recv()

    def product(which, piece):
        lines = pl.ds(pl.multiple_of(which * 2 * rows, 2 * rows), 2 * rows)
        return jnp.dot(
            ctx[lines, :], wo[:, piece * cols : (piece + 1) * cols],
            preferred_element_type=jnp.float32,
        ).reshape(2, rows, cols)

    to_partner = []
    to_over = []

    def forward(piece):
        to_partner[piece].wait_recv()
        total = away[piece, core] + take_mate[piece].astype(jnp.float32)
        give_over[piece] = total.astype(jnp.bfloat16)
        copy = remote(
            give_over.at[piece], take_over.at[piece],
            over_send.at[piece], over_recv.at[piece], seq, over,
        )
        copy.start()
        to_over.append(copy)

    for piece in range(pieces):
        away[piece] = product(1 - chip, piece)
        give_mate[piece] = away[piece, 1 - core].astype(jnp.bfloat16)
        copy = remote(
            give_mate.at[piece], take_mate.at[piece],
            sum_send.at[piece], sum_recv.at[piece], seq, mate,
        )
        copy.start()
        to_partner.append(copy)
        if piece:
            forward(piece - 1)
    forward(pieces - 1)

    for copy in incoming[1]:
        copy.wait_recv()
    to_home = []
    for piece in range(pieces):
        home[piece] = product(chip, piece)
        give_home[piece] = home[piece, 1 - core].astype(jnp.bfloat16)
        copy = remote(
            give_home.at[piece], take_home.at[piece],
            home_send.at[piece], home_recv.at[piece], seq, mate,
        )
        copy.start()
        to_home.append(copy)
    for piece in range(pieces):
        to_home[piece].wait_recv()
        to_over[piece].wait_recv()
        total = home[piece, core] + take_home[piece].astype(jnp.float32)
        total = total + take_over[piece].astype(jnp.float32)
        out_ref[:, piece * cols : (piece + 1) * cols] = total.astype(jnp.bfloat16)
    waiting = sent + to_partner + to_over + to_home
    for copy in waiting + [to_mate] + crossing + passing + group_sent + rings[0].sent + rings[1].sent:
        copy.wait_send()


def exchange(normed, w_query, w_key, w_value, w_out, pattern, slide_lengths):
    rows, width = normed.shape
    depth = w_out.shape[0]
    pieces = 4
    cols = width // pieces
    span = 4 * rows
    kept = 4 * KEPT
    any_spec = pl.BlockSpec(memory_space=pltpu.HBM)
    vmem_spec = pl.BlockSpec(memory_space=pltpu.VMEM)
    dma = pltpu.SemaphoreType.DMA
    vmem = pltpu.VMEM
    sums = vmem((pieces, 2, rows, cols), jnp.float32)
    parts = vmem((pieces, rows, cols), jnp.bfloat16)
    return pl.pallas_call(
        exchange_kernel,
        out_shape=jax.ShapeDtypeStruct((rows, width), jnp.bfloat16),
        in_specs=[pl.BlockSpec(memory_space=pltpu.SMEM)] + [any_spec] * 5 + [vmem_spec],
        out_specs=vmem_spec,
        scratch_shapes=[
            vmem((4, rows, width), jnp.bfloat16),
            vmem((6, width, 256), jnp.bfloat16),
            vmem((NY, 2, 3, span // 2, HEAD), jnp.bfloat16),
            vmem((NY, KEPT, BLOCK), jnp.bfloat16),
            vmem((2, NY, kept, HEAD), jnp.bfloat16),
            vmem((2, NZ, NX, NY, kept, HEAD), jnp.bfloat16),
            vmem((NY, 2, 3, span // 2, HEAD), jnp.bfloat16),
            vmem((8 + NY, span, 2 * HEAD), jnp.bfloat16),
            vmem((8 + NY, HEAD + 16, span), jnp.bfloat16),
            vmem((NY, 2 * HEAD, span), jnp.bfloat16),
            vmem((NY, HEAD + 16, span), jnp.float32),
            vmem((NY, 8, span), jnp.float32),
            vmem((NY, span, HEAD), jnp.bfloat16),
            vmem((span, depth), jnp.bfloat16),
            vmem((depth, width), jnp.bfloat16),
            sums, sums, parts, parts, parts, parts, parts, parts,
            dma, dma((6,)), dma((2,)), dma((2,)),
            dma, dma, dma((ROW_CUTS,)), dma((ROW_CUTS,)), dma((ROW_CUTS,)), dma((ROW_CUTS,)),
            dma((4 * NY,)), dma((4 * NY,)), dma((2 * NY,)), dma((4 * 2 * NZ,)), dma((80,)),
            dma, dma, dma((2 * NY,)), dma((2 * NY,)),
            dma((pieces,)), dma((pieces,)), dma((pieces,)), dma((pieces,)),
            dma((pieces,)), dma((pieces,)),
        ],
        compiler_params=pltpu.CompilerParams(
            collective_id=0, has_side_effects=True, vmem_limit_bytes=67043328
        ),
        name="exchange",
    )(slide_lengths, normed, w_query, w_key, w_value, w_out, pattern)


def shards(normed, w_query, w_key, w_value, w_out, pattern, slide_lengths):
    return exchange(normed, w_query, w_key, w_value, w_out, pattern, slide_lengths)


def solution(mesh):
    placed = (
        P(("seq", "sub"), None),
        P(None, "sub"),
        P(None, "sub"),
        P(None, "sub"),
        P("sub", None),
        P("sub", None),
        P(),
    )
    return jax.shard_map(
        shards, mesh=mesh, in_specs=placed, out_specs=P(("seq", "sub"), None), check_vma=False
    )
```
